128 devices in a mesh: expert: 64 (over y, x, z), zero: 2 (over core).
Axes of the slice: x: 4, y: 4, z: 4, core: 2. Of those that a mesh axis runs over, the one named last changes fastest.
Arguments:
- tokens: bfloat16 [8192, 7168], P(('expert', 'zero')), may hold values from -6 to 6
- expert_ids: int32 [8192, 8], P(('expert', 'zero')), may hold values from 0 to 63, all different within a row; in each aligned block of 64 rows (0 to 63, 64 to 127, ...) at most 10 rows name the same one
- gate_logits: float32 [8192, 8], P(('expert', 'zero')), may hold values from -6 to 6
- w_gate: bfloat16 [64, 7168, 1024], P('expert', 'zero'), may hold values from -0.0625 to 0.0625
- w_up: bfloat16 [64, 7168, 1024], P('expert', 'zero'), may hold values from -0.0625 to 0.0625
- w_down: bfloat16 [64, 1024, 7168], P('expert', None, 'zero'), may hold values from -0.1875 to 0.1875
Outputs:
- moe_out: bfloat16 [8192, 7168], P(('expert', 'zero'))
The draws below stay inside these ranges and needn't reach their ends.
Inputs may be any that keep to these rules, and one draw needn't show every extreme that they name: `expert_ids`: in each aligned block of 64 tokens (the tokens of one device) no expert is named by more than 10 tokens, and in some block one expert is named by exactly 10. Each token names 8 different experts, and every expert is named somewhere.
All inputs are finite; a program needn't handle non-finite values.
Results may differ from the reference program's by a relative error of at most 0.0059.
Values may be sent and summed in bfloat16 or wider, within the bound.
No kernel may reach another device: no remote copies, remote signals or barrier semaphores. Data moves between devices by JAX's collectives and lax.ppermute only.
A program may use at most 256 MiB of HBM per device.

```python
import math
import jax
import jax.numpy as jnp
import numpy as np
from jax import lax

D = 7168
TOP_K = 8
HW = 1024
TOK_DEV = 64
EXPERTS = 64
TOKENS = 8192
CAP = 10
N_EXPERT = 64
N_ZERO = 2


def shard_levels(stream_key, extent, pieces, low, top_value):
    loudness, own = 1.0, jax.random.fold_in(stream_key, 6)
    for dim, parts in pieces:
        heights = jnp.exp(jax.random.uniform(jax.random.fold_in(own, dim), (parts,), jnp.float32, low / len(pieces), top_value / len(pieces)))
        loudness = loudness * jnp.repeat(heights, extent[dim] // parts).reshape([-1 if axis == dim else 1 for axis in range(len(extent))])
    return loudness


def deal_out(rng, own, number, rows, number_of, top, reach, lean):
    ranking = jax.random.permutation(rng, number_of)
    heavy_load, ordinary = shares(number_of, rows * top, reach, lean, True), shares(number_of, rows * top, reach, lean, False)
    places = jnp.arange(number_of)

    def named(sizes, rotation):
        used = int((sizes > 0).sum())
        fixed = max(1, used // 4)
        shifted = fixed + (places - fixed + rotation * (used - fixed)) % max(1, number_of - fixed)
        return jnp.zeros((number_of,), jnp.int32).at[ranking[jnp.where(places < fixed, places, shifted)]].set(jnp.asarray(sizes, jnp.int32))

    sizes = jnp.where(number % 4 == 0, named(heavy_load, number // 4), named(ordinary, number - number // 4 - 1))
    mixed = jax.random.permutation(jax.random.fold_in(own, 3), number_of)
    giver, sink = mixed[0:number_of // 2 * 2:2], mixed[1:number_of // 2 * 2:2]
    room = jnp.minimum(sizes[giver] - 1, reach - sizes[sink]) // 2
    room = jnp.where((giver == ranking[0]) | (sink == ranking[0]) | (sizes[sink] == 0), 0, jnp.maximum(room, 0))
    shifted = jax.random.randint(jax.random.fold_in(own, 4), (number_of // 2,), 0, 1 << 20) % (room + 1)
    sizes = sizes.at[giver].add(-shifted).at[sink].add(shifted)
    labels = jnp.searchsorted(jnp.cumsum(sizes), jnp.arange(rows * top), side="right").astype(jnp.int32)
    listing = labels.reshape(top, rows).T
    listing = listing[jax.random.permutation(jax.random.fold_in(own, 1), rows)]
    rotation = jax.random.randint(jax.random.fold_in(own, 2), (rows, 1), 0, top)
    return jnp.take_along_axis(listing, (jnp.arange(top)[None, :] + rotation) % top, axis=1)


def shares(count, total, limit, lean, full):
    loads = [(1 << 20) // math.isqrt(grade ** lean) + 1 for grade in range(1, count + 1)]
    largest = limit if full else min(limit, max(-(-total // count), total * loads[0] // sum(loads)))
    least = 1 if total - largest >= count - 1 else 0
    given, spare = [largest] + [least] * (count - 1), total - largest - least * (count - 1)
    while spare > 0:
        candidates = [i for i in range(1, count) if given[i] < largest] or [i for i in range(1, count) if given[i] < limit]
        mass, budget = sum([loads[i] for i in candidates]), spare
        for i in candidates:
            extra = min(limit - given[i], max(1, budget * loads[i] // mass), spare)
            given[i] = given[i] + extra
            spare = spare - extra
    return np.array(given)


def bell_draw(key, shape, width, limit, cuts=(), dtype=jnp.bfloat16):
    factor_of = shard_levels(key, shape, cuts, -0.22, 0.18) if cuts else 1.0
    result = jax.random.normal(key, shape, jnp.float32) * width * factor_of
    return jnp.minimum(jnp.maximum(result, -limit), limit).astype(dtype)


def setup_inputs(seed: int = 0) -> dict:
    arg_keys = jax.random.split(jax.random.key(seed), 7)
    tokens = bell_draw(arg_keys[0], (TOKENS, D), 1.0, 6.0, ((0, 128),))
    expert_ids_keys = jax.random.split(jax.random.fold_in(arg_keys[1], 1), TOKENS // TOK_DEV)
    expert_ids_turns = jax.random.permutation(jax.random.fold_in(arg_keys[1], 3), TOKENS // TOK_DEV)
    expert_ids = jax.vmap(lambda own, number: deal_out(jax.random.fold_in(arg_keys[1], 2), own, number, TOK_DEV, EXPERTS, TOP_K, CAP, 2))(expert_ids_keys, expert_ids_turns).reshape((TOKENS, TOP_K))
    gate_logits = bell_draw(arg_keys[2], (TOKENS, TOP_K), 1.5, 6.0, ((0, 128),), jnp.float32)
    w_gate = bell_draw(arg_keys[3], (EXPERTS, D, HW), D ** -0.5, 0.0625, ((0, 64), (1, 2)))
    w_up = bell_draw(arg_keys[4], (EXPERTS, D, HW), D ** -0.5, 0.0625, ((0, 64), (1, 2)))
    w_down = bell_draw(arg_keys[5], (EXPERTS, HW, D), HW ** -0.5, 0.1875, ((0, 64), (2, 2)))
    return {"tokens": tokens, "expert_ids": expert_ids, "gate_logits": gate_logits, "w_gate": w_gate, "w_up": w_up, "w_down": w_down}


ROUTE_SCALE = 2.5


def reference(tokens, expert_ids, gate_logits, w_gate, w_up, w_down):
    scores = jax.nn.sigmoid(gate_logits)
    weights = ROUTE_SCALE * scores / jnp.sum(scores, axis=1, keepdims=True)
    flat_ids = expert_ids.reshape(-1)
    flat_weights = weights.reshape(-1)
    row_limit = N_EXPERT * N_ZERO * CAP

    def one_expert(expert, output_sum):
        matches = flat_ids == expert
        located = jnp.nonzero(matches, size=row_limit, fill_value=0)[0].astype(jnp.int32)
        is_live = jnp.arange(row_limit) < jnp.sum(matches.astype(jnp.int32))
        owners = located // TOP_K
        row_data = tokens[owners]
        gate_pre = jnp.dot(row_data, w_gate[expert], preferred_element_type=jnp.float32)
        up_pre = jnp.dot(row_data, w_up[expert], preferred_element_type=jnp.float32)
        activated = (jax.nn.silu(gate_pre) * up_pre).astype(jnp.bfloat16)
        outputs = jnp.dot(activated, w_down[expert], preferred_element_type=jnp.float32).astype(jnp.bfloat16)
        scale_rows = jnp.where(is_live, flat_weights[located], jnp.zeros_like(flat_weights[located]))
        return output_sum.at[owners].add(scale_rows[:, None] * outputs.astype(jnp.float32))

    total_out = lax.fori_loop(0, EXPERTS, one_expert, jnp.zeros(tokens.shape, jnp.float32))
    return total_out.astype(jnp.bfloat16)
```

```python
import jax
import jax.numpy as jnp
from jax import lax
from jax.experimental import pallas as pl
from jax.experimental.pallas import tpu as pltpu
from jax.sharding import PartitionSpec as P

ROUTE_SCALE = 2.5
MAIN = 8
REST = 2
FOLD = MAIN // REST
F32, BF16 = jnp.float32, jnp.bfloat16


def slot_table(ids_ref, experts, tok_count):
    row = lax.broadcasted_iota(jnp.int32, (experts, tok_count), 0)
    chosen = jnp.zeros((experts, tok_count), F32)
    for k in range(ids_ref.shape[0]):
        chosen = chosen + jnp.where(ids_ref[k : k + 1, :] == row, 1.0, 0.0)
    earlier = (
        lax.broadcasted_iota(jnp.int32, (tok_count, tok_count), 0)
        < lax.broadcasted_iota(jnp.int32, (tok_count, tok_count), 1)
    ).astype(F32)
    rank = jnp.dot(chosen.astype(BF16), earlier.astype(BF16), preferred_element_type=F32)
    slot = jnp.where(chosen > 0, rank, -1.0)
    return jnp.broadcast_to(slot[:, None, :], (experts, MAIN, tok_count)).reshape(experts * MAIN, tok_count)


def slot_masks(slot):
    sub = lax.broadcasted_iota(jnp.int32, slot.shape, 0) % MAIN
    main = slot == sub.astype(F32)
    rest = slot == (MAIN + sub % REST).astype(F32)
    return main, [rest & (sub // REST == j) for j in range(FOLD)]


def pack_body(ids_ref, tok_ref, out_ref, sel_ref, *, experts):
    step = pl.program_id(0)
    width = out_ref.shape[1]
    tok_count = tok_ref.shape[0]

    @pl.when(step == 0)
    def _():
        main, rest = slot_masks(slot_table(ids_ref, experts, tok_count))
        for n, mask in enumerate([main] + rest):
            sel_ref[n] = jnp.where(mask, 1.0, 0.0).astype(BF16)

    @pl.when(step < FOLD)
    def _():
        cols = tok_ref[:, pl.ds(pl.multiple_of(step * width, 128), width)]
        out_ref[...] = jnp.dot(sel_ref[0], cols, preferred_element_type=F32).astype(BF16)

    @pl.when(step == FOLD)
    def _():
        total = jnp.dot(sel_ref[1], tok_ref[:, :width], preferred_element_type=F32)
        for j in range(1, FOLD):
            total += jnp.dot(sel_ref[1 + j], tok_ref[:, j * width : (j + 1) * width], preferred_element_type=F32)
        out_ref[...] = total.astype(BF16)


def pack(ids_t, tokens, experts):
    tok_count, model = tokens.shape
    width = model // FOLD
    rows = experts * MAIN
    return pl.pallas_call(
        lambda *refs: pack_body(*refs, experts=experts),
        grid=(FOLD + 1,),
        in_specs=[
            pl.BlockSpec(ids_t.shape, lambda i: (0, 0)),
            pl.BlockSpec(tokens.shape, lambda i: (0, 0)),
        ],
        out_specs=pl.BlockSpec((rows, width), lambda i: (0, i)),
        out_shape=jax.ShapeDtypeStruct((rows, model + width), BF16),
        scratch_shapes=[pltpu.VMEM((1 + FOLD, rows, tok_count), BF16)],
        name="pack_rows",
    )(ids_t, tokens)


def folding(rows, j):
    count = rows // FOLD
    whole = lax.broadcasted_iota(jnp.int32, (count, rows), 0)
    folded = lax.broadcasted_iota(jnp.int32, (count, rows), 1)
    target = (whole // REST) * MAIN + j * REST + whole % REST
    return jnp.where(folded == target, 1.0, 0.0).astype(BF16)


def ffn_body(x_ref, left_ref, wg_ref, wu_ref, wd_ref, out_ref, gate_ref, up_ref, act_ref, fold_ref, *, parts):
    step = pl.program_id(0)
    rows = x_ref.shape[0]
    width = x_ref.shape[1]
    k_steps = FOLD * parts

    @pl.when(step < k_steps)
    def _():
        j, h = step // parts, step % parts
        left = left_ref[:, pl.ds(pl.multiple_of(h * width, 128), width)]
        extra = jnp.dot(folding(rows, j), left, preferred_element_type=F32).astype(BF16)
        x = jnp.concatenate([x_ref[...], extra], axis=0)
        gate = jnp.dot(x, wg_ref[...], preferred_element_type=F32)
        up = jnp.dot(x, wu_ref[...], preferred_element_type=F32)

        @pl.when(step == 0)
        def _():
            gate_ref[...] = gate
            up_ref[...] = up

        @pl.when(step > 0)
        def _():
            gate_ref[...] += gate
            up_ref[...] += up

    @pl.when(step == k_steps)
    def _():
        gate = gate_ref[...]
        act_ref[...] = ((gate / (1.0 + jnp.exp(-gate))) * up_ref[...]).astype(BF16)
        fold_ref[...] = jnp.zeros(fold_ref.shape, BF16)

    @pl.when((step >= k_steps) & (step < 2 * k_steps))
    def _():
        j, h = (step - k_steps) // parts, (step - k_steps) % parts
        y = jnp.dot(act_ref[...], wd_ref[...], preferred_element_type=F32).astype(BF16)
        out_ref[...] = y[:rows]
        back = lax.dot_general(
            folding(rows, j), y[rows:], (((0,), (0,)), ((), ())), preferred_element_type=F32
        ).astype(BF16)
        cols = pl.ds(pl.multiple_of(h * width, 128), width)
        fold_ref[:, cols] = fold_ref[:, cols] + back

    @pl.when(step >= 2 * k_steps)
    def _():
        h = step - 2 * k_steps
        out_ref[...] = fold_ref[:, pl.ds(pl.multiple_of(h * width, 128), width)]


def ffn(x, w_gate, w_up, w_down, parts=2):
    rows, total = x.shape
    model, hidden = w_gate.shape
    fold_width = model // FOLD
    width = fold_width // parts
    k_steps = FOLD * parts
    all_rows = rows + rows // FOLD
    return pl.pallas_call(
        lambda *refs: ffn_body(*refs, parts=parts),
        grid=(2 * k_steps + parts,),
        in_specs=[
            pl.BlockSpec((rows, width), lambda i: (0, jnp.minimum(i, k_steps - 1))),
            pl.BlockSpec((rows, fold_width), lambda i: (0, FOLD)),
            pl.BlockSpec((width, hidden), lambda i: (jnp.minimum(i, k_steps - 1), 0)),
            pl.BlockSpec((width, hidden), lambda i: (jnp.minimum(i, k_steps - 1), 0)),
            pl.BlockSpec((hidden, width), lambda i: (0, jnp.clip(i - k_steps, 0, k_steps - 1))),
        ],
        out_specs=pl.BlockSpec((rows, width), lambda i: (0, jnp.maximum(i - k_steps, 0))),
        out_shape=jax.ShapeDtypeStruct((rows, total), BF16),
        scratch_shapes=[
            pltpu.VMEM((all_rows, hidden), F32),
            pltpu.VMEM((all_rows, hidden), F32),
            pltpu.VMEM((all_rows, hidden), BF16),
            pltpu.VMEM((rows, fold_width), BF16),
        ],
        compiler_params=pltpu.CompilerParams(vmem_limit_bytes=56 * 1024 * 1024),
        name="expert_ffn",
    )(x, x, w_gate, w_up, w_down)


def merge_body(ids_ref, logit_ref, y_ref, left_ref, out_ref, mix_ref, *, experts):
    step = pl.program_id(0)
    tok_count = out_ref.shape[0]

    @pl.when(step == 0)
    def _():
        scores = 1.0 / (1.0 + jnp.exp(-logit_ref[...]))
        weights = ROUTE_SCALE * scores / jnp.sum(scores, axis=0, keepdims=True)
        row = lax.broadcasted_iota(jnp.int32, (experts, tok_count), 0)
        gain = jnp.zeros((experts, tok_count), F32)
        for k in range(ids_ref.shape[0]):
            gain = gain + jnp.where(ids_ref[k : k + 1, :] == row, weights[k : k + 1, :], 0.0)
        gain = jnp.broadcast_to(gain[:, None, :], (experts, MAIN, tok_count)).reshape(experts * MAIN, tok_count)
        main, rest = slot_masks(slot_table(ids_ref, experts, tok_count))
        for n, mask in enumerate([main] + rest):
            part = jnp.where(mask, gain, 0.0)
            high = part.astype(BF16).astype(F32)
            both = jnp.concatenate([high, part - high], axis=1)
            mix_ref[n] = both.T.astype(BF16)

    total = jnp.dot(mix_ref[0], y_ref[...], preferred_element_type=F32)
    total += jnp.dot(mix_ref[1 + step], left_ref[...], preferred_element_type=F32)
    out_ref[...] = (total[:tok_count] + total[tok_count:]).astype(BF16)


def merge(ids_t, logits_t, y, experts):
    tok_count = ids_t.shape[1]
    rows, total = y.shape
    width = total // (FOLD + 1)
    return pl.pallas_call(
        lambda *refs: merge_body(*refs, experts=experts),
        grid=(FOLD,),
        in_specs=[
            pl.BlockSpec(ids_t.shape, lambda i: (0, 0)),
            pl.BlockSpec(logits_t.shape, lambda i: (0, 0)),
            pl.BlockSpec((rows, width), lambda i: (0, i)),
            pl.BlockSpec((rows, width), lambda i: (0, FOLD)),
        ],
        out_specs=pl.BlockSpec((tok_count, width), lambda i: (0, i)),
        out_shape=jax.ShapeDtypeStruct((tok_count, width * FOLD), BF16),
        scratch_shapes=[pltpu.VMEM((1 + FOLD, 2 * tok_count, rows), BF16)],
        name="merge_rows",
    )(ids_t, logits_t, y, y)


def exchange(x, experts):
    rows, total = x.shape
    out = lax.all_to_all(x.reshape(experts, rows // experts, total), "expert", split_axis=0, concat_axis=0, tiled=True)
    return out.reshape(rows, total)


def shards(tokens, expert_ids, gate_logits, w_gate, w_up, w_down):
    experts = lax.axis_size("expert")
    ids_t, logits_t = expert_ids.T, gate_logits.T
    gate_full = lax.all_gather(w_gate[0], "zero", axis=0, tiled=True)
    up_full = lax.all_gather(w_up[0], "zero", axis=0, tiled=True)
    down_full = lax.all_gather(w_down[0], "zero", axis=1, tiled=True)
    arrived = exchange(pack(ids_t, tokens, experts), experts)
    results = ffn(arrived, gate_full, up_full, down_full)
    return merge(ids_t, logits_t, exchange(results, experts), experts)


def solution(mesh):
    return jax.shard_map(
        shards,
        mesh=mesh,
        in_specs=(
            P(("expert", "zero"), None),
            P(("expert", "zero"), None),
            P(("expert", "zero"), None),
            P("expert", "zero", None),
            P("expert", "zero", None),
            P("expert", None, "zero"),
        ),
        out_specs=P(("expert", "zero"), None),
        check_vma=False,
    )
```

```python
import jax
import jax.numpy as jnp
from jax import lax
from jax.experimental import pallas as pl
from jax.experimental.pallas import tpu as pltpu
from jax.sharding import PartitionSpec as P


ROUTE_SCALE = 2.5
MAIN = 8
REST = 2
FOLD = MAIN // REST
F32, BF16 = jnp.float32, jnp.bfloat16


def slot_table(ids_ref, experts, tok_count):
    row = lax.broadcasted_iota(jnp.int32, (experts, tok_count), 0)
    chosen = jnp.zeros((experts, tok_count), F32)
    for k in range(ids_ref.shape[0]):
        chosen = chosen + jnp.where(ids_ref[k : k + 1, :] == row, 1.0, 0.0)
    earlier = (
        lax.broadcasted_iota(jnp.int32, (tok_count, tok_count), 0)
        < lax.broadcasted_iota(jnp.int32, (tok_count, tok_count), 1)
    ).astype(F32)
    rank = jnp.dot(chosen.astype(BF16), earlier.astype(BF16), preferred_element_type=F32)
    slot = jnp.where(chosen > 0, rank, -1.0)
    return jnp.broadcast_to(slot[:, None, :], (experts, MAIN, tok_count)).reshape(experts * MAIN, tok_count)


def slot_masks(slot):
    sub = lax.broadcasted_iota(jnp.int32, slot.shape, 0) % MAIN
    main = slot == sub.astype(F32)
    rest = slot == (MAIN + sub % REST).astype(F32)
    return main, [rest & (sub // REST == j) for j in range(FOLD)]


def pack_body(ids_ref, tok_ref, out_ref, sel_ref, all_ref, *, experts):
    step = pl.program_id(0)
    width = out_ref.shape[1]
    tok_count = tok_ref.shape[0]

    @pl.when(step == 0)
    def _():
        main, rest = slot_masks(slot_table(ids_ref, experts, tok_count))
        sel_ref[...] = jnp.where(main, 1.0, 0.0).astype(BF16)
        all_ref[...] = jnp.concatenate([jnp.where(mask, 1.0, 0.0) for mask in rest], axis=1).astype(BF16)

    @pl.when(step < FOLD)
    def _():
        cols = tok_ref[:, pl.ds(pl.multiple_of(step * width, 128), width)]
        out_ref[...] = jnp.dot(sel_ref[...], cols, preferred_element_type=F32).astype(BF16)

    @pl.when(step == FOLD)
    def _():
        stack = jnp.concatenate([tok_ref[:, j * width : (j + 1) * width] for j in range(FOLD)], axis=0)
        out_ref[...] = jnp.dot(all_ref[...], stack, preferred_element_type=F32).astype(BF16)


def pack(ids_t, tokens, experts):
    tok_count, model = tokens.shape
    width = model // FOLD
    rows = experts * MAIN
    return pl.pallas_call(
        lambda *refs: pack_body(*refs, experts=experts),
        grid=(FOLD + 1,),
        in_specs=[
            pl.BlockSpec(ids_t.shape, lambda i: (0, 0)),
            pl.BlockSpec(tokens.shape, lambda i: (0, 0)),
        ],
        out_specs=pl.BlockSpec((rows, width), lambda i: (0, i)),
        out_shape=jax.ShapeDtypeStruct((rows, model + width), BF16),
        scratch_shapes=[pltpu.VMEM((rows, tok_count), BF16), pltpu.VMEM((rows, FOLD * tok_count), BF16)],
        name="pack_rows",
    )(ids_t, tokens)


def folding(rows, j):
    count = rows // FOLD
    whole = lax.broadcasted_iota(jnp.int32, (count, rows), 0)
    folded = lax.broadcasted_iota(jnp.int32, (count, rows), 1)
    target = (whole // REST) * MAIN + j * REST + whole % REST
    return jnp.where(folded == target, 1.0, 0.0).astype(BF16)


def ffn_body(z_ref, x_ref, left_ref, g0, g1, u0, u1, d0, d1, out_ref, gate_ref, up_ref, act_ref, fold_ref, in_ref, down_ref, in_sem, down_sem):
    step = pl.program_id(0)
    rows, width = x_ref.shape
    half = FOLD // 2
    cut = (width // 512) * 256
    pieces = ((0, cut), (cut, width - cut))
    z = z_ref[0]

    def project_copies(source, first, slot):
        return [
            pltpu.make_async_copy(
                source[n].at[pl.ds(first + at, size)], in_ref.at[slot, n, pl.ds(at, size)], in_sem.at[slot, n, p]
            )
            for p, (at, size) in enumerate(pieces)
            for n in range(2)
        ]

    def expand_copy(source, first, slot):
        return pltpu.make_async_copy(source.at[:, pl.ds(first, width)], down_ref.at[slot], down_sem.at[slot])

    def start(block):
        if block < FOLD:
            source = (g0, u0) if block < half else (g1, u1)
            for copy in project_copies(source, (block % half) * width, block % 2):
                copy.start()
        else:
            source = d0 if block - FOLD < half else d1
            expand_copy(source, (block % half) * width, block % 2).start()

    @pl.when(step == 0)
    def _():
        start(0)

    for block in range(1, 2 * FOLD):
        @pl.when(step == block - 1)
        def _(block=block):
            start(block)

    slot = step % 2

    def place_of(i):
        return jnp.where(i < half, z * half + i, (1 - z) * half + i - half)

    @pl.when(step < FOLD)
    def _():
        extra = jnp.dot(folding(rows, place_of(step)), left_ref[...], preferred_element_type=F32).astype(BF16)
        x = jnp.concatenate([x_ref[...], extra], axis=0)
        copies = project_copies((g0, u0), 0, slot)
        total = [None, None]
        for p, (at, size) in enumerate(pieces):
            for n in range(2):
                copies[2 * p + n].wait()
            for n in range(2):
                part = jnp.dot(x[:, at : at + size], in_ref[slot, n, at : at + size], preferred_element_type=F32)
                total[n] = part if p == 0 else total[n] + part

        @pl.when(step == 0)
        def _():
            gate_ref[...] = total[0]
            up_ref[...] = total[1]

        @pl.when(step > 0)
        def _():
            gate_ref[...] += total[0]
            up_ref[...] += total[1]

    @pl.when(step == FOLD)
    def _():
        gate = gate_ref[...]
        act_ref[...] = ((gate / (1.0 + jnp.exp(-gate))) * up_ref[...]).astype(BF16)
        fold_ref[...] = jnp.zeros(fold_ref.shape, BF16)

    @pl.when((step >= FOLD) & (step < 2 * FOLD))
    def _():
        expand_copy(d0, 0, slot).wait()
        y = jnp.dot(act_ref[...], down_ref[slot], preferred_element_type=F32).astype(BF16)
        out_ref[...] = y[:rows]
        back = lax.dot_general(
            folding(rows, place_of(step - FOLD)), y[rows:], (((0,), (0,)), ((), ())), preferred_element_type=F32
        )
        fold_ref[...] += back.astype(BF16)

    @pl.when(step == 2 * FOLD)
    def _():
        out_ref[...] = fold_ref[...]


def ffn(place, x, weights):
    rows, total = x.shape
    (g0, g1), (u0, u1), (d0, d1) = weights
    hidden = g0.shape[1]
    half = FOLD // 2
    width = g0.shape[0] // half
    all_rows = rows + rows // FOLD

    def place_of(i, z_ref):
        z = z_ref[0]
        return jnp.where(i < half, z * half + i, (1 - z) * half + i - half)

    def out_place(i, z_ref):
        return jnp.where(i >= 2 * FOLD, FOLD, place_of(jnp.clip(i - FOLD, 0, FOLD - 1), z_ref))

    whole = pl.BlockSpec(memory_space=pl.ANY)
    return pl.pallas_call(
        ffn_body,
        grid_spec=pltpu.PrefetchScalarGridSpec(
            num_scalar_prefetch=1,
            grid=(2 * FOLD + 1,),
            in_specs=[
                pl.BlockSpec((rows, width), lambda i, z_ref: (0, place_of(jnp.minimum(i, FOLD - 1), z_ref))),
                pl.BlockSpec((rows, width), lambda i, z_ref: (0, FOLD)),
                *[whole] * 6,
            ],
            out_specs=pl.BlockSpec((rows, width), lambda i, z_ref: (0, out_place(i, z_ref))),
            scratch_shapes=[
                pltpu.VMEM((all_rows, hidden), F32),
                pltpu.VMEM((all_rows, hidden), F32),
                pltpu.VMEM((all_rows, hidden), BF16),
                pltpu.VMEM((rows, width), BF16),
                pltpu.VMEM((2, 2, width, hidden), BF16),
                pltpu.VMEM((2, hidden, width), BF16),
                pltpu.SemaphoreType.DMA((2, 2, 2)),
                pltpu.SemaphoreType.DMA((2,)),
            ],
        ),
        out_shape=jax.ShapeDtypeStruct((rows, total), BF16),
        compiler_params=pltpu.CompilerParams(vmem_limit_bytes=58 * 1024 * 1024),
        name="expert_ffn",
    )(place, x, x, g0, g1, u0, u1, d0, d1)


def merge_body(ids_ref, logit_ref, y_ref, left_ref, out_ref, mix_ref, *, experts):
    step = pl.program_id(0)
    tok_count = out_ref.shape[0]

    @pl.when(step == 0)
    def _():
        scores = 1.0 / (1.0 + jnp.exp(-logit_ref[...]))
        weights = ROUTE_SCALE * scores / jnp.sum(scores, axis=0, keepdims=True)
        row = lax.broadcasted_iota(jnp.int32, (experts, tok_count), 0)
        gain = jnp.zeros((experts, tok_count), F32)
        for k in range(ids_ref.shape[0]):
            gain = gain + jnp.where(ids_ref[k : k + 1, :] == row, weights[k : k + 1, :], 0.0)
        gain = jnp.broadcast_to(gain[:, None, :], (experts, MAIN, tok_count)).reshape(experts * MAIN, tok_count)
        main, rest = slot_masks(slot_table(ids_ref, experts, tok_count))
        for n, mask in enumerate([main] + rest):
            part = jnp.where(mask, gain, 0.0)
            high = part.astype(BF16).astype(F32)
            both = jnp.concatenate([high, part - high], axis=1)
            mix_ref[n] = both.T.astype(BF16)

    total = jnp.dot(mix_ref[0], y_ref[...], preferred_element_type=F32)
    total += jnp.dot(mix_ref[1 + step], left_ref[...], preferred_element_type=F32)
    out_ref[...] = (total[:tok_count] + total[tok_count:]).astype(BF16)


def merge(ids_t, logits_t, y, experts):
    tok_count = ids_t.shape[1]
    rows, total = y.shape
    width = total // (FOLD + 1)
    return pl.pallas_call(
        lambda *refs: merge_body(*refs, experts=experts),
        grid=(FOLD,),
        in_specs=[
            pl.BlockSpec(ids_t.shape, lambda i: (0, 0)),
            pl.BlockSpec(logits_t.shape, lambda i: (0, 0)),
            pl.BlockSpec((rows, width), lambda i: (0, i)),
            pl.BlockSpec((rows, width), lambda i: (0, FOLD)),
        ],
        out_specs=pl.BlockSpec((tok_count, width), lambda i: (0, i)),
        out_shape=jax.ShapeDtypeStruct((tok_count, width * FOLD), BF16),
        scratch_shapes=[pltpu.VMEM((1 + FOLD, 2 * tok_count, rows), BF16)],
        name="merge_rows",
    )(ids_t, logits_t, y, y)


def exchange(x, experts):
    rows, total = x.shape
    out = lax.all_to_all(x.reshape(experts, rows // experts, total), "expert", split_axis=0, concat_axis=0, tiled=True)
    return out.reshape(rows, total)


def shards(tokens, expert_ids, gate_logits, w_gate, w_up, w_down):
    experts = lax.axis_size("expert")
    place = lax.axis_index("zero").astype(jnp.int32).reshape(1)
    place, tokens = lax.optimization_barrier((place, tokens))
    ids_t, logits_t = expert_ids.T, gate_logits.T
    swap = [(0, 1), (1, 0)]
    weights = []
    for w in (w_gate, w_up, w_down):
        weights.append((w[0], lax.ppermute(w[0], "zero", swap)))
    packed = pack(ids_t, tokens, experts)
    arrived = exchange(packed, experts)
    results = ffn(place, arrived, weights)
    returned = exchange(results, experts)
    return merge(ids_t, logits_t, returned, experts)


def solution(mesh):
    return jax.shard_map(
        shards,
        mesh=mesh,
        in_specs=(
            P(("expert", "zero"), None),
            P(("expert", "zero"), None),
            P(("expert", "zero"), None),
            P("expert", "zero", None),
            P("expert", "zero", None),
            P("expert", None, "zero"),
        ),
        out_specs=P(("expert", "zero"), None),
        check_vma=False,
    )
```

```python
import jax
import jax.numpy as jnp
from jax import lax
from jax.experimental import pallas as pl
from jax.experimental.pallas import tpu as pltpu
from jax.sharding import PartitionSpec as P


ROUTE_SCALE = 2.5
MAIN = 8
REST = 2
FOLD = MAIN // REST
F32, BF16 = jnp.float32, jnp.bfloat16


def slots_of(ids_ref, experts, tok_count):
    row = lax.broadcasted_iota(jnp.int32, (experts, tok_count), 0)
    chosen = jnp.zeros((experts, tok_count), F32)
    for k in range(ids_ref.shape[0]):
        chosen = chosen + jnp.where(ids_ref[k : k + 1, :] == row, 1.0, 0.0)
    earlier = (
        lax.broadcasted_iota(jnp.int32, (tok_count, tok_count), 0)
        < lax.broadcasted_iota(jnp.int32, (tok_count, tok_count), 1)
    ).astype(F32)
    rank = jnp.dot(chosen.astype(BF16), earlier.astype(BF16), preferred_element_type=F32)
    return jnp.where(chosen > 0, rank, -1.0)


def slot_table(ids_ref, experts, tok_count):
    slot = slots_of(ids_ref, experts, tok_count)
    return jnp.broadcast_to(slot[:, None, :], (experts, MAIN, tok_count)).reshape(experts * MAIN, tok_count)


def slot_masks(slot, axis=0):
    sub = lax.broadcasted_iota(jnp.int32, slot.shape, axis) % MAIN
    main = slot == sub.astype(F32)
    rest = slot == (MAIN + sub % REST).astype(F32)
    return main, [rest & (sub // REST == j) for j in range(FOLD)]


def pack_body(ids_ref, tok_ref, out_ref, sel_ref, all_ref, *, experts):
    step = pl.program_id(0)
    width = out_ref.shape[1]
    tok_count = tok_ref.shape[0]

    @pl.when(step == 0)
    def _():
        main, rest = slot_masks(slot_table(ids_ref, experts, tok_count))
        sel_ref[...] = jnp.where(main, 1.0, 0.0).astype(BF16)
        all_ref[...] = jnp.concatenate([jnp.where(mask, 1.0, 0.0) for mask in rest], axis=1).astype(BF16)

    @pl.when(step < FOLD)
    def _():
        cols = tok_ref[:, pl.ds(pl.multiple_of(step * width, 128), width)]
        out_ref[...] = jnp.dot(sel_ref[...], cols, preferred_element_type=F32).astype(BF16)

    @pl.when(step == FOLD)
    def _():
        stack = jnp.concatenate([tok_ref[:, j * width : (j + 1) * width] for j in range(FOLD)], axis=0)
        out_ref[...] = jnp.dot(all_ref[...], stack, preferred_element_type=F32).astype(BF16)


def pack(ids_t, tokens, experts):
    tok_count, model = tokens.shape
    width = model // FOLD
    rows = experts * MAIN
    return pl.pallas_call(
        lambda *refs: pack_body(*refs, experts=experts),
        grid=(FOLD + 1,),
        in_specs=[
            pl.BlockSpec(ids_t.shape, lambda i: (0, 0)),
            pl.BlockSpec(tokens.shape, lambda i: (0, 0)),
        ],
        out_specs=pl.BlockSpec((rows, width), lambda i: (0, i)),
        out_shape=jax.ShapeDtypeStruct((rows, model + width), BF16),
        scratch_shapes=[pltpu.VMEM((rows, tok_count), BF16), pltpu.VMEM((rows, FOLD * tok_count), BF16)],
        compiler_params=pltpu.CompilerParams(vmem_limit_bytes=14 * 1024 * 1024),
        name="pack_rows",
    )(ids_t, tokens)


def folding(rows, back):
    count = rows // FOLD
    whole = lax.broadcasted_iota(jnp.int32, (rows, rows), 1 if back else 0)
    folded = lax.broadcasted_iota(jnp.int32, (rows, rows), 0 if back else 1)
    of_block = whole % count
    target = (of_block // REST) * MAIN + (whole // count) * REST + of_block % REST
    return jnp.where(folded == target, 1.0, 0.0).astype(BF16)


def ffn_body(z_ref, x_ref, left_ref, g0, g1, u0, u1, d0, d1, out_ref, gate_ref, up_ref, act_ref, fold_ref, in_ref, down_ref, in_sem, down_sem):
    step = pl.program_id(0)
    rows, width = x_ref.shape
    half = FOLD // 2
    cut = (width // 512) * 256
    pieces = ((0, cut), (cut, width - cut))
    z = z_ref[0]

    def project_copies(source, first, slot):
        return [
            pltpu.make_async_copy(
                source[n].at[pl.ds(first + at, size)], in_ref.at[slot, n, pl.ds(at, size)], in_sem.at[slot, n, p]
            )
            for p, (at, size) in enumerate(pieces)
            for n in range(2)
        ]

    def expand_copy(source, first, slot):
        return pltpu.make_async_copy(source.at[:, pl.ds(first, width)], down_ref.at[slot], down_sem.at[slot])

    def start(block):
        if block < FOLD:
            source = (g0, u0) if block < half else (g1, u1)
            for copy in project_copies(source, (block % half) * width, block % 2):
                copy.start()
        else:
            source = d0 if block - FOLD < half else d1
            expand_copy(source, (block % half) * width, block % 2).start()

    @pl.when(step == 0)
    def _():
        start(0)
        fold_ref[...] = jnp.dot(folding(rows, False), left_ref[...], preferred_element_type=F32).astype(BF16)

    for block in range(1, 2 * FOLD):
        @pl.when(step == block - 1)
        def _(block=block):
            start(block)

    slot = step % 2

    def place_of(i):
        return jnp.where(i < half, z * half + i, (1 - z) * half + i - half)

    def rows_of(block):
        return pl.ds(pl.multiple_of(block * (rows // FOLD), 16), rows // FOLD)

    @pl.when(step < FOLD)
    def _():
        x = jnp.concatenate([x_ref[...], fold_ref[rows_of(place_of(step)), :]], axis=0)
        copies = project_copies((g0, u0), 0, slot)
        total = [None, None]
        for p, (at, size) in enumerate(pieces):
            for n in range(2):
                copies[2 * p + n].wait()
            for n in range(2):
                part = jnp.dot(x[:, at : at + size], in_ref[slot, n, at : at + size], preferred_element_type=F32)
                total[n] = part if p == 0 else total[n] + part

        @pl.when(step == 0)
        def _():
            gate_ref[...] = total[0]
            up_ref[...] = total[1]

        @pl.when(step > 0)
        def _():
            gate_ref[...] += total[0]
            up_ref[...] += total[1]

    @pl.when(step == FOLD)
    def _():
        gate = gate_ref[...]
        act_ref[...] = ((gate / (1.0 + jnp.exp(-gate))) * up_ref[...]).astype(BF16)

    @pl.when((step >= FOLD) & (step < 2 * FOLD))
    def _():
        expand_copy(d0, 0, slot).wait()
        y = jnp.dot(act_ref[...], down_ref[slot], preferred_element_type=F32).astype(BF16)
        out_ref[...] = y[:rows]
        fold_ref[rows_of(place_of(step - FOLD)), :] = y[rows:]

    @pl.when(step == 2 * FOLD)
    def _():
        out_ref[...] = jnp.dot(folding(rows, True), fold_ref[...], preferred_element_type=F32).astype(BF16)


def ffn(place, x, weights):
    rows, total = x.shape
    (g0, g1), (u0, u1), (d0, d1) = weights
    hidden = g0.shape[1]
    half = FOLD // 2
    width = g0.shape[0] // half
    all_rows = rows + rows // FOLD

    def place_of(i, z_ref):
        z = z_ref[0]
        return jnp.where(i < half, z * half + i, (1 - z) * half + i - half)

    def out_place(i, z_ref):
        return jnp.where(i >= 2 * FOLD, FOLD, place_of(jnp.clip(i - FOLD, 0, FOLD - 1), z_ref))

    whole = pl.BlockSpec(memory_space=pl.ANY)
    return pl.pallas_call(
        ffn_body,
        grid_spec=pltpu.PrefetchScalarGridSpec(
            num_scalar_prefetch=1,
            grid=(2 * FOLD + 1,),
            in_specs=[
                pl.BlockSpec((rows, width), lambda i, z_ref: (0, place_of(jnp.minimum(i, FOLD - 1), z_ref))),
                pl.BlockSpec((rows, width), lambda i, z_ref: (0, FOLD)),
                *[whole] * 6,
            ],
            out_specs=pl.BlockSpec((rows, width), lambda i, z_ref: (0, out_place(i, z_ref))),
            scratch_shapes=[
                pltpu.VMEM((all_rows, hidden), F32),
                pltpu.VMEM((all_rows, hidden), F32),
                pltpu.VMEM((all_rows, hidden), BF16),
                pltpu.VMEM((rows, width), BF16),
                pltpu.VMEM((2, 2, width, hidden), BF16),
                pltpu.VMEM((2, hidden, width), BF16),
                pltpu.SemaphoreType.DMA((2, 2, 2)),
                pltpu.SemaphoreType.DMA((2,)),
            ],
        ),
        out_shape=jax.ShapeDtypeStruct((rows, total), BF16),
        compiler_params=pltpu.CompilerParams(vmem_limit_bytes=48 * 1024 * 1024),
        name="expert_ffn",
    )(place, x, x, g0, g1, u0, u1, d0, d1)


def merge_body(ids_ref, logit_ref, y_ref, left_ref, out_ref, mix_ref, rest_ref, *, experts):
    step = pl.program_id(0)
    tok_count = out_ref.shape[0]

    @pl.when(step == 0)
    def _():
        scores = 1.0 / (1.0 + jnp.exp(-logit_ref[...]))
        weights = ROUTE_SCALE * scores / jnp.sum(scores, axis=0, keepdims=True)
        row = lax.broadcasted_iota(jnp.int32, (experts, tok_count), 0)
        gain = jnp.zeros((experts, tok_count), F32)
        for k in range(ids_ref.shape[0]):
            gain = gain + jnp.where(ids_ref[k : k + 1, :] == row, weights[k : k + 1, :], 0.0)
        high = gain.astype(BF16).astype(F32)
        lanes = (experts, experts * MAIN)
        widen = (
            lax.broadcasted_iota(jnp.int32, lanes, 1) // MAIN == lax.broadcasted_iota(jnp.int32, lanes, 0)
        ).astype(F32).astype(BF16)

        def wide(value):
            return jnp.dot(value.T.astype(BF16), widen, preferred_element_type=F32)

        slot = wide(slots_of(ids_ref, experts, tok_count))
        gains = wide(high), wide(gain - high)
        main, rest = slot_masks(slot, axis=1)

        def spread(masks):
            return jnp.concatenate([jnp.where(mask, part, 0.0) for mask in masks for part in gains], axis=0).astype(BF16)

        mix_ref[...] = spread([main])
        rest_ref[...] = jnp.dot(spread(rest), left_ref[...], preferred_element_type=F32)

    total = jnp.dot(mix_ref[...], y_ref[...], preferred_element_type=F32)
    total += rest_ref[pl.ds(pl.multiple_of(step * 2 * tok_count, 8), 2 * tok_count), :]
    out_ref[...] = (total[:tok_count] + total[tok_count:]).astype(BF16)


def merge(ids_t, logits_t, y, experts):
    tok_count = ids_t.shape[1]
    rows, total = y.shape
    width = total // (FOLD + 1)
    return pl.pallas_call(
        lambda *refs: merge_body(*refs, experts=experts),
        grid=(FOLD,),
        in_specs=[
            pl.BlockSpec(ids_t.shape, lambda i: (0, 0)),
            pl.BlockSpec(logits_t.shape, lambda i: (0, 0)),
            pl.BlockSpec((rows, width), lambda i: (0, i)),
            pl.BlockSpec((rows, width), lambda i: (0, FOLD)),
        ],
        out_specs=pl.BlockSpec((tok_count, width), lambda i: (0, i)),
        out_shape=jax.ShapeDtypeStruct((tok_count, width * FOLD), BF16),
        scratch_shapes=[pltpu.VMEM((2 * tok_count, rows), BF16), pltpu.VMEM((FOLD * 2 * tok_count, width), F32)],
        compiler_params=pltpu.CompilerParams(vmem_limit_bytes=20 * 1024 * 1024),
        name="merge_rows",
    )(ids_t, logits_t, y, y)


def exchange(x, experts):
    rows, total = x.shape
    out = lax.all_to_all(x.reshape(experts, rows // experts, total), "expert", split_axis=0, concat_axis=0, tiled=True)
    return out.reshape(rows, total)


def shards(tokens, expert_ids, gate_logits, w_gate, w_up, w_down):
    experts = lax.axis_size("expert")
    place = lax.axis_index("zero").astype(jnp.int32).reshape(1)
    place, tokens = lax.optimization_barrier((place, tokens))
    ids_t, logits_t = expert_ids.T, gate_logits.T
    swap = [(0, 1), (1, 0)]
    weights = []
    for w in (w_gate, w_up, w_down):
        weights.append((w[0], lax.ppermute(w[0], "zero", swap)))
    packed = pack(ids_t, tokens, experts)
    arrived = exchange(packed, experts)
    results = ffn(place, arrived, weights)
    returned = exchange(results, experts)
    return merge(ids_t, logits_t, returned, experts)


def solution(mesh):
    return jax.shard_map(
        shards,
        mesh=mesh,
        in_specs=(
            P(("expert", "zero"), None),
            P(("expert", "zero"), None),
            P(("expert", "zero"), None),
            P("expert", "zero", None),
            P("expert", "zero", None),
            P("expert", None, "zero"),
        ),
        out_specs=P(("expert", "zero"), None),
        check_vma=False,
    )
```
